32 devices in a mesh: seq: 4 (over z), tok: 8 (over y, x, core).
Axes of the slice: x: 2, y: 2, z: 4, core: 2. Of those that a mesh axis runs over, the one named last changes fastest.
Arguments:
- tokens: bfloat16 [4, 4, 2048, 768], P(None, 'seq', 'tok'), may hold values from -6 to 6
- cotangent: bfloat16 [4, 4, 2048, 768], P(None, 'seq', 'tok'), may hold values from -6 to 6
- documents: int32 [4, 4, 2048], P(None, 'seq', 'tok'), may hold values from 0 to 7, never falling along the last dimension, each value on 1 to 1536 neighbouring positions
- positions: int32 [4, 4, 16], P(None, 'seq', 'tok'), may hold values from 0 to 63
- inner_mixing: bfloat16 [768, 2304], P(('seq', 'tok')), may hold values from -0.21875 to 0.21875
- inner_output: bfloat16 [768, 768], P(('seq', 'tok')), may hold values from -0.875 to 0.875
- inner_expand: bfloat16 [768, 3072], P(('seq', 'tok')), may hold values from -0.21875 to 0.21875
- inner_shrink: bfloat16 [3072, 768], P(('seq', 'tok')), may hold values from -0.15625 to 0.15625
- inner_lift: bfloat16 [3072], P(('seq', 'tok')), may hold values from -3 to 3
- inner_shifts: bfloat16 [6, 768], P(None, ('seq', 'tok')), may hold values from -3 to 3
- inner_gains: bfloat16 [2, 768], P(None, ('seq', 'tok')), may hold values from 0.5 to 1.5
- outer_mixing: bfloat16 [768, 2304], P(('seq', 'tok')), may hold values from -0.21875 to 0.21875
- outer_output: bfloat16 [768, 768], P(('seq', 'tok')), may hold values from -0.875 to 0.875
- outer_expand: bfloat16 [768, 3072], P(('seq', 'tok')), may hold values from -0.21875 to 0.21875
- outer_shrink: bfloat16 [3072, 768], P(('seq', 'tok')), may hold values from -0.15625 to 0.15625
- outer_lift: bfloat16 [3072], P(('seq', 'tok')), may hold values from -3 to 3
- outer_shifts: bfloat16 [6, 768], P(None, ('seq', 'tok')), may hold values from -3 to 3
- outer_gains: bfloat16 [2, 768], P(None, ('seq', 'tok')), may hold values from 0.5 to 1.5
- position_table: bfloat16 [64, 768], P(None, ('seq', 'tok')), may hold values from -5 to 5
Outputs:
- output: bfloat16 [4, 4, 2048, 768], P(None, 'seq', 'tok')
- tokens_gradient: bfloat16 [4, 4, 2048, 768], P(None, 'seq', 'tok')
- inner_mixing_gradient: float32 [768, 2304], P(('seq', 'tok'))
- inner_output_gradient: float32 [768, 768], P(('seq', 'tok'))
- inner_expand_gradient: float32 [768, 3072], P(('seq', 'tok'))
- inner_shrink_gradient: float32 [3072, 768], P(('seq', 'tok'))
- inner_lift_gradient: float32 [3072], P(('seq', 'tok'))
- inner_shifts_gradient: float32 [6, 768], P(None, ('seq', 'tok'))
- inner_gains_gradient: float32 [2, 768], P(None, ('seq', 'tok'))
- outer_mixing_gradient: float32 [768, 2304], P(('seq', 'tok'))
- outer_output_gradient: float32 [768, 768], P(('seq', 'tok'))
- outer_expand_gradient: float32 [768, 3072], P(('seq', 'tok'))
- outer_shrink_gradient: float32 [3072, 768], P(('seq', 'tok'))
- outer_lift_gradient: float32 [3072], P(('seq', 'tok'))
- outer_shifts_gradient: float32 [6, 768], P(None, ('seq', 'tok'))
- outer_gains_gradient: float32 [2, 768], P(None, ('seq', 'tok'))
- position_table_gradient: float32 [64, 768], P(None, ('seq', 'tok'))
The draws below stay inside these ranges and needn't reach their ends.
Inputs may be any that keep to these rules, and one draw needn't show every extreme that they name: `documents`: within each sequence the document numbers never fall along the positions; each document holds 1 to 1536 consecutive tokens and one holds exactly 1536.
All inputs are finite; a program needn't handle non-finite values.
Results may differ from the reference program's by a relative error of at most 0.028.
Values may be sent and summed in bfloat16 or wider, within the bound.
No kernel may reach another device: no remote copies, remote signals or barrier semaphores. Data moves between devices by JAX's collectives and lax.ppermute only.
A program may use at most 320 MiB of HBM per device.

```python
import math
import jax
import jax.numpy as jnp
import numpy as np
from jax import lax

D = 768
H = 12
HD = 64
FF = 3072
SEG = 128
SEGPOS = 64
MB = 4
SEQ_MB = 4
SLOTS = 16
LEN = 2048
DOCS = 8
DOC_MOST = 1536


def touch_ends(values, rng, low, largest):
    longest = values.shape.index(max(values.shape))
    spots = []
    for shift in (0, 1):
        where = [jax.random.randint(jax.random.fold_in(rng, axis), (), 0, length) for axis, length in enumerate(values.shape)]
        where[longest] = (where[longest] + shift) % values.shape[longest]
        spots.append(tuple(where))
    return values.at[spots[0]].set(low).at[spots[1]].set(largest)


def strengthened(values, stream_key, source, target, shards_of, factor):
    owner, partner = [(jnp.arange(values.shape[position]) // (values.shape[position] // shards_of)).reshape([-1 if axis == position else 1 for axis in range(values.ndim)]) for position in (source, target)]
    chosen = jax.random.permutation(stream_key, shards_of)[partner]
    strong = (owner == chosen) | (owner == (partner + shards_of // 2) % shards_of)
    return jnp.where(strong, factor * values, values)


def block_scale(rng, extent, split, low, largest):
    def one(dim, blocks):
        draws = jax.random.uniform(jax.random.fold_in(jax.random.fold_in(rng, 6), dim), (blocks,), jnp.float32, low / len(split), largest / len(split))
        return jnp.repeat(jnp.exp(draws), extent[dim] // blocks).reshape((-1,) + (1,) * (len(extent) - dim - 1))

    level = one(*split[0])
    for cut in split[1:]:
        level = level * one(*cut)
    return level


def length_profile(number_of, total, reach, lean):
    portions = [(1 << 20) // math.isqrt(rank ** lean) + 1 for rank in range(2, number_of + 1)]
    rest, given = total - reach - (number_of - 1), [1] * (number_of - 1)
    while rest > 0:
        free = [i for i in range(number_of - 1) if given[i] < reach]
        pool, left = sum([portions[i] for i in free]), rest
        for i in free:
            addition = min(reach - given[i], max(1, left * portions[i] // pool), rest)
            given[i] = given[i] + addition
            rest = rest - addition
    return np.array([reach] + given)


def ragged(rng, amount, total, reach, lean):
    if amount == 2:
        one = jax.random.randint(rng, (), max(1, total - reach), min(reach, total - 1) + 1)
        return jnp.stack([one, total - one])
    lengths = jnp.asarray(length_profile(amount, total, reach, lean), jnp.int32)
    pairs = (amount - 1) // 2
    giver, taker = lengths[1:1 + 2 * pairs:2], lengths[2:2 + 2 * pairs:2]
    slack = jnp.minimum(giver - 1, reach - taker)
    moved = jax.random.randint(jax.random.fold_in(rng, 1), (pairs,), 0, 1 << 20) % (slack + 1)
    lengths = lengths.at[1:1 + 2 * pairs:2].set(giver - moved).at[2:2 + 2 * pairs:2].set(taker + moved)
    return lengths[jax.random.permutation(jax.random.fold_in(rng, 2), amount)]


def centred(key, shape, width, bound, shards=(), held_as=jnp.bfloat16):
    values = width * jax.random.normal(key, shape, jnp.float32)
    if shards:
        values = values * block_scale(key, shape, shards, -0.22, 0.18)
    return jnp.clip(values, -bound, bound).astype(held_as)


def heavy_noise(rng, shape, width, bound, shards, heavy, kind=jnp.bfloat16):
    drawn = width * jax.random.normal(rng, shape, jnp.float32)
    if shards:
        drawn = drawn * block_scale(rng, shape, shards, -0.22, 0.18)
    return jnp.clip(strengthened(drawn, jax.random.fold_in(rng, 3), *heavy), -bound, bound).astype(kind)


def setup_inputs(seed: int = 0) -> dict:
    key_of = jax.random.split(jax.random.key(seed), 20)
    tokens = heavy_noise(key_of[0], (MB, SEQ_MB, LEN, D), 1.0, 6.0, ((1, 4), (2, 8)), (2, 3, 8, 2.0))
    cotangent = centred(key_of[1], (MB, SEQ_MB, LEN, D), 1.0, 6.0, ((1, 4), (2, 8)))
    documents = jax.vmap(lambda own: jnp.searchsorted(jnp.cumsum(ragged(own, DOCS, LEN, DOC_MOST, 2)), jnp.arange(LEN), side="right"))(jax.random.split(key_of[2], MB * SEQ_MB)).reshape((MB, SEQ_MB, LEN)).astype(jnp.int32)
    positions = touch_ends(jax.random.randint(key_of[3], (MB, SEQ_MB, SLOTS), 0, SEGPOS), jax.random.fold_in(key_of[3], 1), 0, SEGPOS - 1).astype(jnp.int32)
    inner_mixing = centred(key_of[4], (D, 3 * D), D ** -0.5, 0.21875, ((0, 32),))
    inner_output = centred(key_of[5], (D, D), (D // 16) ** -0.5, 0.875, ((0, 32),))
    inner_expand = centred(key_of[6], (D, FF), D ** -0.5, 0.21875, ((0, 32),))
    inner_shrink = centred(key_of[7], (FF, D), (FF // 2) ** -0.5, 0.15625, ((0, 32),))
    inner_lift = centred(key_of[8], (FF,), 0.5, 3.0, ((0, 32),))
    inner_shifts = centred(key_of[9], (6, D), 0.5, 3.0, ((1, 32),))
    inner_gains = jnp.clip(1.0 + 0.1 * jax.random.normal(key_of[10], (2, D), jnp.float32), 0.5, 1.5).astype(jnp.bfloat16)
    outer_mixing = centred(key_of[11], (D, 3 * D), D ** -0.5, 0.21875, ((0, 32),))
    outer_output = centred(key_of[12], (D, D), (D // 16) ** -0.5, 0.875, ((0, 32),))
    outer_expand = centred(key_of[13], (D, FF), D ** -0.5, 0.21875, ((0, 32),))
    outer_shrink = centred(key_of[14], (FF, D), (FF // 2) ** -0.5, 0.15625, ((0, 32),))
    outer_lift = centred(key_of[15], (FF,), 0.5, 3.0, ((0, 32),))
    outer_shifts = centred(key_of[16], (6, D), 0.5, 3.0, ((1, 32),))
    outer_gains = jnp.clip(1.0 + 0.1 * jax.random.normal(key_of[17], (2, D), jnp.float32), 0.5, 1.5).astype(jnp.bfloat16)
    position_table = centred(key_of[18], (SEGPOS, D), 1.0, 5.0, ((1, 32),))
    return dict(tokens=tokens, cotangent=cotangent, documents=documents, positions=positions, inner_mixing=inner_mixing, inner_output=inner_output, inner_expand=inner_expand, inner_shrink=inner_shrink, inner_lift=inner_lift, inner_shifts=inner_shifts, inner_gains=inner_gains, outer_mixing=outer_mixing, outer_output=outer_output, outer_expand=outer_expand, outer_shrink=outer_shrink, outer_lift=outer_lift, outer_shifts=outer_shifts, outer_gains=outer_gains, position_table=position_table)


HIGH = lax.Precision.HIGHEST
EPS = 1e-05
NEGATIVE = -1e+30

@jax.custom_vjp
def low(v):
    return lax.optimization_barrier(v.astype(jnp.bfloat16)).astype(jnp.float32)

@jax.custom_vjp
def low_back(v):
    return v

def low_keep(v):
    return (low(v), None)

def low_pass(kept, grad):
    return (grad,)

def back_keep(v):
    return (v, None)

def back_low(kept, grad):
    return (low(grad),)
low.defvjp(low_keep, low_pass)
low_back.defvjp(back_keep, back_low)

def normalize(value, gain, shift):
    centered = value - lax.optimization_barrier(jnp.mean(value, -1, keepdims=True))
    return centered * lax.rsqrt(lax.optimization_barrier(jnp.mean(centered * centered, -1, keepdims=True)) + EPS) * gain + shift

def weigh(scores, allowed):
    return low(jax.nn.softmax(jnp.where(allowed, low_back(scores), NEGATIVE), axis=-1))

def block(start, parts, mixer):
    mixing, output, expand, shrink, lift, shifts, gains = parts
    joined = low_back(jnp.dot(low(start), mixing, precision=HIGH))
    query = low((joined[:, :D] + shifts[0]) * HD ** (-0.5))
    key = low(joined[:, D:2 * D])
    value = low(joined[:, 2 * D:] + shifts[1])
    mixed = low(low_back(mixer(query, key, value)))
    middle = normalize(start + low_back(jnp.dot(mixed, output, precision=HIGH)) + shifts[2], gains[0], shifts[4])
    raised = low_back(jnp.dot(low(middle), expand, precision=HIGH)) + lift
    shaped = low(jax.nn.gelu(raised, approximate=False))
    lowered = low_back(jnp.dot(shaped, shrink, precision=HIGH)) + shifts[3]
    return normalize(middle + lowered, gains[1], shifts[5])

def sequence(start, docs, places, inner, outer, table):
    slot_ids = docs.reshape(SLOTS, SEG)
    within_allowed = (slot_ids[:, :, None] == slot_ids[:, None, :])[:, None]
    shape = (SLOTS, SEG, H, HD)

    def within(query, key, value):
        scores = jnp.einsum('aqhd,akhd->ahqk', query.reshape(shape), key.reshape(shape), precision=HIGH)
        mixed = jnp.einsum('ahqk,akhd->aqhd', weigh(scores, within_allowed), value.reshape(shape), precision=HIGH)
        return mixed.reshape(LEN, D)
    leading = slot_ids[:, 0]
    cross_allowed = (leading[:, None] == leading[None, :])[None]
    narrow = (SLOTS, H, HD)

    def across(query, key, value):
        scores = jnp.einsum('qhd,khd->hqk', query.reshape(narrow), key.reshape(narrow), precision=HIGH)
        mixed = jnp.einsum('hqk,khd->qhd', weigh(scores, cross_allowed), value.reshape(narrow), precision=HIGH)
        return mixed.reshape(SLOTS, D)
    hidden = block(start, inner, within)
    grouped = hidden.reshape(SLOTS, SEG, D)
    summary = block(grouped[:, 0] + table[places], outer, across)
    return jnp.concatenate([summary[:, None], grouped[:, 1:]], 1).reshape(LEN, D)

def reference(tokens, cotangent, documents, positions, inner_mixing, inner_output, inner_expand, inner_shrink, inner_lift, inner_shifts, inner_gains, outer_mixing, outer_output, outer_expand, outer_shrink, outer_lift, outer_shifts, outer_gains, position_table):
    inner = tuple((part.astype(jnp.float32) for part in (inner_mixing, inner_output, inner_expand, inner_shrink, inner_lift, inner_shifts, inner_gains)))
    outer = tuple((part.astype(jnp.float32) for part in (outer_mixing, outer_output, outer_expand, outer_shrink, outer_lift, outer_shifts, outer_gains)))
    table = position_table.astype(jnp.float32)
    count = MB * SEQ_MB
    starts = tokens.reshape(count, LEN, D).astype(jnp.float32)
    docs = documents.reshape(count, LEN)
    places = positions.reshape(count, SLOTS)

    def forward(starts, inner, outer, table):

        def single(items):
            return sequence(items[0], items[1], items[2], inner, outer, table)
        return lax.map(jax.checkpoint(single), (starts, docs, places))
    result, pull = jax.vjp(forward, starts, inner, outer, table)
    start_grad, inner_grad, outer_grad, table_grad = pull(cotangent.reshape(count, LEN, D).astype(jnp.float32))
    shape = (MB, SEQ_MB, LEN, D)
    return (result.reshape(shape).astype(jnp.bfloat16), start_grad.reshape(shape).astype(jnp.bfloat16), inner_grad[0], inner_grad[1], inner_grad[2], inner_grad[3], inner_grad[4], inner_grad[5], inner_grad[6], outer_grad[0], outer_grad[1], outer_grad[2], outer_grad[3], outer_grad[4], outer_grad[5], outer_grad[6], table_grad)
```

```python
import jax
import jax.numpy as jnp
from jax import lax
from jax.experimental import pallas as pl
from jax.experimental.pallas import tpu as pltpu
from jax.sharding import PartitionSpec as P

H = 12
HD = 64
SEG = 128
LANES = 128

EPS = 1e-05
NEGATIVE = -1e30
ROOT_HALF = 0.7071067811865476
INVERSE_ROOT_TAU = 0.3989422804014327
F32 = jnp.float32
BF16 = jnp.bfloat16
ALL = ("seq", "tok")


def product(left, right):
    return jnp.dot(left, right, preferred_element_type=F32)


def across(left, right):
    return lax.dot_general(left, right, (((0,), (0,)), ((), ())), preferred_element_type=F32)


def against(left, right):
    return lax.dot_general(left, right, (((1,), (1,)), ((), ())), preferred_element_type=F32)


def unit_of(value):
    centered = value - jnp.mean(value, -1, keepdims=True)
    factor = lax.rsqrt(jnp.mean(centered * centered, -1, keepdims=True) + EPS)
    return centered * factor, factor


def unit_back(delta, gain, unit, factor):
    scaled = delta * gain
    return factor * (
        scaled
        - jnp.mean(scaled, -1, keepdims=True)
        - unit * jnp.mean(scaled * unit, -1, keepdims=True)
    )


def gelu_parts(value):
    phi = 0.5 * (1.0 + lax.erf(value * ROOT_HALF))
    return value * phi, phi + value * jnp.exp(-0.5 * value * value) * INVERSE_ROOT_TAU


def two_heads(pair, low):
    zero = jnp.zeros_like(pair)
    return jnp.concatenate([jnp.where(low, pair, zero), jnp.where(low, zero, pair)], 0)


def attend_kernel(qkv_ref, col_ref, row_ref, o_ref, p_ref):
    width = o_ref.shape[1]
    low = lax.broadcasted_iota(jnp.int32, (SEG, LANES), 1) < HD
    allowed = col_ref[...] == row_ref[0]
    allowed = jnp.concatenate([allowed, allowed], 0)
    for pair in range(width // LANES):
        at = pair * LANES
        query = two_heads(qkv_ref[:, at : at + LANES], low)
        key = qkv_ref[:, width + at : width + at + LANES]
        value = qkv_ref[:, 2 * width + at : 2 * width + at + LANES]
        scores = jnp.where(allowed, against(query, key), NEGATIVE)
        weight = jnp.exp(scores - jnp.max(scores, -1, keepdims=True))
        weight = (weight / jnp.sum(weight, -1, keepdims=True)).astype(BF16)
        p_ref[0, pair] = weight
        mixed = product(weight, value)
        o_ref[:, at : at + LANES] = jnp.where(low, mixed[:SEG], mixed[SEG:]).astype(BF16)


def attend(qkv, col, row, width):
    rows = qkv.shape[0]
    segments = rows // SEG
    pairs = width // LANES
    return pl.pallas_call(
        attend_kernel,
        grid=(segments,),
        in_specs=[
            pl.BlockSpec((SEG, 3 * width), lambda i: (i, 0)),
            pl.BlockSpec((SEG, 1), lambda i: (i, 0)),
            pl.BlockSpec((1, 1, SEG), lambda i: (i, 0, 0)),
        ],
        out_specs=[
            pl.BlockSpec((SEG, width), lambda i: (i, 0)),
            pl.BlockSpec((1, pairs, 2 * SEG, SEG), lambda i: (i, 0, 0, 0)),
        ],
        out_shape=[
            jax.ShapeDtypeStruct((rows, width), BF16),
            jax.ShapeDtypeStruct((segments, pairs, 2 * SEG, SEG), BF16),
        ],
        cost_estimate=pl.CostEstimate(
            flops=8 * rows * SEG * width, bytes_accessed=rows * width * 10, transcendentals=rows * SEG * H
        ),
        name="attend",
    )(qkv, col, row)


def attend_back_kernel(qkv_ref, p_ref, delta_ref, eb_ref, qsum_ref, vsum_ref):
    width = delta_ref.shape[1]
    low = lax.broadcasted_iota(jnp.int32, (SEG, LANES), 1) < HD

    @pl.when(pl.program_id(0) == 0)
    def _():
        qsum_ref[...] = jnp.zeros_like(qsum_ref)
        vsum_ref[...] = jnp.zeros_like(vsum_ref)

    for pair in range(width // LANES):
        at = pair * LANES
        query = two_heads(qkv_ref[:, at : at + LANES], low)
        key = qkv_ref[:, width + at : width + at + LANES]
        value = qkv_ref[:, 2 * width + at : 2 * width + at + LANES]
        delta = two_heads(delta_ref[:, at : at + LANES], low)
        weight_low = p_ref[0, pair]
        weight = weight_low.astype(F32)
        pressure = against(delta, value)
        moved = weight * (pressure - jnp.sum(weight * pressure, -1, keepdims=True))
        moved = moved.astype(BF16)
        query_delta = product(moved, key)
        query_delta = jnp.where(low, query_delta[:SEG], query_delta[SEG:]) * HD ** (-0.5)
        key_delta = across(moved, query)
        value_delta = across(weight_low, delta)
        eb_ref[:, at : at + LANES] = query_delta.astype(BF16)
        eb_ref[:, width + at : width + at + LANES] = key_delta.astype(BF16)
        eb_ref[:, 2 * width + at : 2 * width + at + LANES] = value_delta.astype(BF16)
        qsum_ref[:, at : at + LANES] += jnp.sum(query_delta, 0, keepdims=True)
        vsum_ref[:, at : at + LANES] += jnp.sum(value_delta, 0, keepdims=True)


def attend_back(qkv, weights, delta):
    rows, width = delta.shape
    segments = rows // SEG
    pairs = width // LANES
    return pl.pallas_call(
        attend_back_kernel,
        grid=(segments,),
        in_specs=[
            pl.BlockSpec((SEG, 3 * width), lambda i: (i, 0)),
            pl.BlockSpec((1, pairs, 2 * SEG, SEG), lambda i: (i, 0, 0, 0)),
            pl.BlockSpec((SEG, width), lambda i: (i, 0)),
        ],
        out_specs=[
            pl.BlockSpec((SEG, 3 * width), lambda i: (i, 0)),
            pl.BlockSpec((1, width), lambda i: (0, 0)),
            pl.BlockSpec((1, width), lambda i: (0, 0)),
        ],
        out_shape=[
            jax.ShapeDtypeStruct((rows, 3 * width), BF16),
            jax.ShapeDtypeStruct((1, width), F32),
            jax.ShapeDtypeStruct((1, width), F32),
        ],
        cost_estimate=pl.CostEstimate(
            flops=16 * rows * SEG * width, bytes_accessed=rows * width * 16, transcendentals=0
        ),
        name="attend_back",
    )(qkv, weights, delta)


def cross(qkv, allowed, batches, width):
    q, k, v = (
        qkv[:, part * width : (part + 1) * width].reshape(batches, -1, H, HD) for part in range(3)
    )
    scores = jnp.einsum("aqhd,akhd->ahqk", q, k, preferred_element_type=F32)
    scores = jnp.where(allowed[:, None], scores, NEGATIVE)
    weight = jnp.exp(scores - jnp.max(scores, -1, keepdims=True))
    weight = weight / jnp.sum(weight, -1, keepdims=True)
    weight_low = weight.astype(BF16)
    mixed = jnp.einsum("ahqk,akhd->aqhd", weight_low, v, preferred_element_type=F32)
    return mixed.reshape(-1, width).astype(BF16), (q, k, v, weight, weight_low)


def cross_back(saved, delta, batches, width):
    q, k, v, weight, weight_low = saved
    delta = delta.reshape(batches, -1, H, HD)
    pressure = jnp.einsum("aqhd,akhd->ahqk", delta, v, preferred_element_type=F32)
    moved = weight * (pressure - jnp.sum(weight * pressure, -1, keepdims=True))
    moved = moved.astype(BF16)
    dq = jnp.einsum("ahqk,akhd->aqhd", moved, k, preferred_element_type=F32)
    dk = jnp.einsum("ahqk,aqhd->akhd", moved, q, preferred_element_type=F32)
    dv = jnp.einsum("ahqk,aqhd->akhd", weight_low, delta, preferred_element_type=F32)
    dq, dk, dv = (part.reshape(-1, width) for part in (dq * HD ** (-0.5), dk, dv))
    return jnp.concatenate([dq, dk, dv], 1).astype(BF16), jnp.sum(dq, 0), jnp.sum(dv, 0)


def forward(start, first, parts, mixer):
    mixing, output, expand, shrink, lift, shift, gain = parts
    width = start.shape[1]
    bias = jnp.concatenate([shift[0], jnp.zeros_like(shift[0]), shift[1]])
    scale = jnp.concatenate([jnp.full((width,), HD ** (-0.5), F32), jnp.ones((2 * width,), F32)])
    qkv = ((product(first, mixing) + bias) * scale).astype(BF16)
    mixed, saved = mixer(qkv)
    unit1, factor1 = unit_of(start + product(mixed, output) + shift[2])
    middle = unit1 * gain[0] + shift[4]
    middle_low = middle.astype(BF16)
    shaped, slope = gelu_parts(product(middle_low, expand) + lift)
    shaped = shaped.astype(BF16)
    slope = slope.astype(BF16)
    unit2, factor2 = unit_of(middle + product(shaped, shrink) + shift[3])
    final = unit2 * gain[1] + shift[5]
    return final, (first, saved, mixed, unit1, factor1, middle_low, shaped, slope, unit2, factor2)


def backward(delta, cache, parts, mixer_back):
    mixing, output, expand, shrink, lift, shift, gain = parts
    first, saved, mixed, unit1, factor1, middle_low, shaped, slope, unit2, factor2 = cache
    e2 = unit_back(delta, gain[1], unit2, factor2)
    gain1, shift5, shift3 = jnp.sum(delta * unit2, 0), jnp.sum(delta, 0), jnp.sum(e2, 0)
    e2b = e2.astype(BF16)
    ez = against(e2b, shrink) * slope.astype(F32)
    lift_grad = jnp.sum(ez, 0)
    ezb = ez.astype(BF16)
    dm = e2 + against(ezb, expand)
    e1 = unit_back(dm, gain[0], unit1, factor1)
    gain0, shift4, shift2 = jnp.sum(dm * unit1, 0), jnp.sum(dm, 0), jnp.sum(e1, 0)
    e1b = e1.astype(BF16)
    eb, shift0, shift1 = mixer_back(saved, against(e1b, output).astype(BF16))
    start_delta = e1 + against(eb, mixing)
    shift_grad = jnp.stack([shift0, shift1, shift2, shift3, shift4, shift5])
    gain_grad = jnp.stack([gain0, gain1])
    factors = ((first, eb), (mixed, e1b), (middle_low, ezb), (shaped, e2b))
    return start_delta, factors, (lift_grad, shift_grad, gain_grad)


def per_device(
    tokens,
    cotangent,
    documents,
    positions,
    inner_mixing,
    inner_output,
    inner_expand,
    inner_shrink,
    inner_lift,
    inner_shifts,
    inner_gains,
    outer_mixing,
    outer_output,
    outer_expand,
    outer_shrink,
    outer_lift,
    outer_shifts,
    outer_gains,
    position_table,
):
    batches = tokens.shape[0]
    width = tokens.shape[3]
    rows = batches * tokens.shape[2]
    own = inner_mixing.shape[0]
    hidden = inner_expand.shape[1]
    ratio = hidden // width
    seqs = lax.axis_size("seq")
    toks = lax.axis_size("tok")
    slots = tokens.shape[2] // SEG
    places = position_table.shape[0]
    tok = lax.axis_index("tok")

    def folded(part):
        return jnp.concatenate([part[j * own : (j + 1) * own] for j in range(ratio)], 1)

    def unfolded(part):
        return (
            part.reshape(-1, own, ratio, width).transpose(0, 2, 1, 3).reshape(ratio * width, width)
        )

    small = [
        inner_lift.reshape(own, ratio),
        inner_shifts.T,
        inner_gains.T,
        outer_lift.reshape(own, ratio),
        outer_shifts.T,
        outer_gains.T,
        position_table.T,
    ]
    count = sum(part.shape[1] for part in small)
    small.append(jnp.zeros((own, -count % LANES), BF16))

    lead = lax.all_gather(
        jnp.concatenate([inner_mixing] + small, 1), ALL, axis=0, tiled=True
    )
    rest = lax.all_gather(
        jnp.concatenate([inner_output, inner_expand, folded(inner_shrink)], 1),
        ALL,
        axis=0,
        tiled=True,
    )
    outer_all = lax.all_gather(
        jnp.concatenate([outer_mixing, outer_output, outer_expand, folded(outer_shrink)], 1),
        ALL,
        axis=0,
        tiled=True,
    )
    summary_cotangent = cotangent.reshape(batches, slots, SEG, width)[:, :, 0]
    summary_docs = documents.reshape(batches, slots, SEG)[:, :, :1]
    early = jnp.concatenate(
        [summary_cotangent, jnp.broadcast_to(summary_docs.astype(BF16), (batches, slots, LANES))], 2
    )
    early = lax.all_gather(early, "tok", axis=1, tiled=True)

    small_all = lead[:, 3 * width :].astype(F32)
    at = 0

    def take(columns):
        nonlocal at
        at += columns
        return small_all[:, at - columns : at]

    inner_small = (take(ratio).reshape(hidden), take(6).T, take(2).T)
    outer_small = (take(ratio).reshape(hidden), take(6).T, take(2).T)
    table = lead[:, 3 * width + at : 3 * width + at + places].T
    inner = (
        lead[:, : 3 * width],
        rest[:, :width],
        rest[:, width : width + hidden],
        unfolded(rest[:, width + hidden :]),
    ) + inner_small
    outer = (
        outer_all[:, : 3 * width],
        outer_all[:, 3 * width : 4 * width],
        outer_all[:, 4 * width : 4 * width + hidden],
        unfolded(outer_all[:, 4 * width + hidden :]),
    ) + outer_small

    first = tokens.reshape(rows, width)
    docs = documents.reshape(rows)
    col = docs[:, None]
    row = docs.reshape(-1, 1, SEG)

    def within(qkv):
        mixed, weights = attend(qkv, col, row, width)
        return mixed, (qkv, weights)

    def within_back(saved, delta):
        eb, qsum, vsum = attend_back(saved[0], saved[1], delta)
        return eb, qsum[0], vsum[0]

    h1, cache = forward(first.astype(F32), first, inner, within)
    grouped = h1.reshape(batches, slots, SEG, width)

    picked = (positions.reshape(-1, 1) == jnp.arange(places, dtype=jnp.int32)[None, :]).astype(BF16)
    c_own = grouped[:, :, 0] + product(picked, table).reshape(batches, slots, width)
    c_all = lax.all_gather(
        jnp.concatenate([c_own, picked.astype(F32).reshape(batches, slots, places)], 2)
        if places % LANES == 0
        else jnp.concatenate(
            [
                c_own,
                jnp.pad(
                    picked.astype(F32).reshape(batches, slots, places),
                    ((0, 0), (0, 0), (0, -places % LANES)),
                ),
            ],
            2,
        ),
        "tok",
        axis=1,
        tiled=True,
    )
    count = c_all.shape[1]
    picked_all = c_all[:, :, width : width + places].reshape(batches * count, places)
    c = c_all[:, :, :width].reshape(batches * count, width)
    docs_all = early[:, :, width]
    allowed = docs_all[:, :, None] == docs_all[:, None, :]
    c2, outer_cache = forward(
        c, c.astype(BF16), outer, lambda qkv: cross(qkv, allowed, batches, width)
    )
    dc, outer_factors, outer_sums = backward(
        early[:, :, :width].reshape(batches * count, width).astype(F32),
        outer_cache,
        outer,
        lambda saved, delta: cross_back(saved, delta, batches, width),
    )

    def mine(value):
        parts = value.reshape(value.shape[0], seqs, toks, -1)
        return lax.dynamic_index_in_dim(parts, tok, 2, keepdims=False)

    pieces = []
    for left, right in outer_factors:
        left = mine(left)
        piece = across(left.reshape(left.shape[0], -1), right)
        if left.shape[2] != own:
            piece = piece.reshape(seqs, ratio, own, width).transpose(0, 2, 1, 3)
        pieces.append(piece.reshape(seqs, own, -1))
    table_grad = lax.dot_general(
        picked_all, dc, (((0,), (0,)), ((), ())), precision=lax.Precision.HIGHEST
    )
    lift_grad, shift_grad, gain_grad = outer_sums
    sums = [mine(lift_grad[None]).reshape(seqs, own, ratio)]
    for part in (shift_grad, gain_grad, table_grad):
        sums.append(mine(part).transpose(1, 2, 0))
    sums = jnp.concatenate(sums, 2)
    sums = jnp.pad(sums, ((0, 0), (0, 0), (0, -sums.shape[2] % LANES)))
    outer_total = jnp.concatenate(pieces + [sums], 2).astype(BF16)
    outer_total = lax.psum_scatter(outer_total, "seq", scatter_dimension=0, tiled=False)

    def own_rows(value):
        return lax.dynamic_slice_in_dim(
            value.reshape(batches, count, width), tok * slots, slots, axis=1
        )

    output = (
        jnp.concatenate([own_rows(c2)[:, :, None], grouped[:, :, 1:]], 2)
        .astype(BF16)
        .reshape(tokens.shape)
    )
    incoming = cotangent.astype(F32).reshape(batches, slots, SEG, width)
    delta = jnp.concatenate([own_rows(dc)[:, :, None], incoming[:, :, 1:]], 2).reshape(rows, width)
    dx, factors, sums = backward(delta, cache, inner, within_back)
    tokens_gradient = dx.astype(BF16).reshape(tokens.shape)
    mixing_grad, output_grad, expand_grad, shrink_grad = (
        across(left, right).astype(BF16) for left, right in factors
    )
    lift_grad, shift_grad, gain_grad = sums
    sums = jnp.concatenate([lift_grad.reshape(width, ratio), shift_grad.T, gain_grad.T], 1)
    sums = jnp.pad(sums, ((0, 0), (0, -sums.shape[1] % LANES))).astype(BF16)
    shrink_own = lax.psum_scatter(shrink_grad, ALL, scatter_dimension=0, tiled=True)
    expand_own = lax.psum_scatter(expand_grad, ALL, scatter_dimension=0, tiled=True)
    mixing_own = lax.psum_scatter(mixing_grad, ALL, scatter_dimension=0, tiled=True)
    last = lax.psum_scatter(
        jnp.concatenate([output_grad, sums], 1), ALL, scatter_dimension=0, tiled=True
    )

    def vectors(part):
        return (
            part[:, :ratio].reshape(-1),
            part[:, ratio : ratio + 6].T,
            part[:, ratio + 6 : ratio + 8].T,
        )

    last = last.astype(F32)
    outer_total = outer_total.astype(F32)
    outer_shrink_own = outer_total[:, 4 * width + hidden : 4 * width + 2 * hidden]
    outer_shrink_own = (
        outer_shrink_own.reshape(own, ratio, width).transpose(1, 0, 2).reshape(ratio * own, width)
    )
    outer_sums = outer_total[:, 4 * width + 2 * hidden :]
    return (
        (
            output,
            tokens_gradient,
            mixing_own.astype(F32),
            last[:, :width],
            expand_own.astype(F32),
            shrink_own.astype(F32),
        )
        + vectors(last[:, width:])
        + (
            outer_total[:, : 3 * width],
            outer_total[:, 3 * width : 4 * width],
            outer_total[:, 4 * width : 4 * width + hidden],
            outer_shrink_own,
        )
        + vectors(outer_sums)
        + (outer_sums[:, ratio + 8 : ratio + 8 + places].T,)
    )


ROWS = P(None, "seq", "tok", None)
IDS = P(None, "seq", "tok")
TALL = P(ALL, None)
FLAT = P(ALL)
WIDE = P(None, ALL)
LAYER = (TALL, TALL, TALL, TALL, FLAT, WIDE, WIDE)


def solution(mesh):
    return jax.shard_map(
        per_device,
        mesh=mesh,
        in_specs=(ROWS, ROWS, IDS, IDS) + LAYER + LAYER + (WIDE,),
        out_specs=(ROWS, ROWS) + LAYER + LAYER + (WIDE,),
        check_vma=False,
    )
```
